32 devices in a mesh: rx: 4 (over y, x), chirp: 8 (over z, core).
Axes of the slice: x: 2, y: 2, z: 4, core: 2. Of those that a mesh axis runs over, the one named last changes fastest.
Arguments:
- samples: bfloat16 [2, 128, 128, 4096], P(None, None, 'rx', 'chirp'), may hold values from -6 to 6
- tx_offsets: int32 [12], replicated, may hold values from 0 to 3840, as said below
- band_owner: int32 [16], replicated, may hold values from 0 to 3, as said below
- beam_weights: bfloat16 [2, 256, 1536], replicated, may hold values from -0.109375 to 0.109375
Outputs:
- tile_store: bfloat16 [48, 2, 256, 2048], P('rx', None, None, 'chirp')
The draws below stay inside these ranges and needn't reach their ends.
Inputs may be any that keep to these rules, and one draw needn't show every extreme that they name: `tx_offsets`: each offset is 256 times a Doppler slot of 0 to 15; transmitters use different slots, and slots 0 and 15 are always used. `band_owner`: at most 12 bands share an owner, and one owner has exactly 12.
All inputs are finite; a program needn't handle non-finite values.
Results may differ from the reference program's by a relative error of at most 0.007.
Values may be sent and summed in bfloat16 or wider, within the bound.
No kernel may reach another device: no remote copies, remote signals or barrier semaphores. Data moves between devices by JAX's collectives and lax.ppermute only.
A program may use at most 192 MiB of HBM per device.

```python
import math
import jax
import jax.numpy as jnp
from jax import lax

TX = 12
RX = 128
K1 = 64
K2 = 64
K = 4096
SLOTS = 16
V = 256
BANDS = 16
BW = 16
B = 256
CHANNELS = 1536
RANGE = 128
CAP = 12
N_RX = 4


def draw_tx_offsets(key, part):
    first_key, second_key = jax.random.split(jax.random.fold_in(key, 11))
    middle = 1 + jax.random.permutation(first_key, SLOTS - 2)[:TX - 2]
    chosen = jnp.concatenate([jnp.array([0, SLOTS - 1], jnp.int32), middle.astype(jnp.int32)])
    shuffle = jax.random.permutation(second_key, TX)
    return (chosen[shuffle] * V).astype(jnp.int32)


def draw_band_owner(key, part):
    first_key, second_key, third_key = jax.random.split(jax.random.fold_in(key, 23), 3)
    busiest = jax.random.randint(first_key, (), 0, N_RX)
    band_order = jax.random.permutation(second_key, BANDS)
    others = jax.random.permutation(third_key, N_RX - 1)
    position = jnp.arange(BANDS, dtype=jnp.int32)
    rest_owner = (busiest + 1 + others[(position - CAP) % (N_RX - 1)]) % N_RX
    owner_by_position = jnp.where(position < CAP, busiest, rest_owner).astype(jnp.int32)
    return jnp.zeros((BANDS,), jnp.int32).at[band_order].set(owner_by_position)


def steps_of(stream_key, shape, shards, low, largest):
    loudness = 1.0
    for dim, shards_of in shards:
        steps = jax.random.uniform(jax.random.fold_in(jax.random.fold_in(stream_key, 6), dim), (shards_of,), jnp.float32, low / len(shards), largest / len(shards))
        loudness = loudness * jnp.repeat(jnp.exp(steps), shape[dim] // shards_of).reshape((-1,) + (1,) * (len(shape) - 1 - dim))
    return loudness


def gaussian(rng, extent, spread, reach, shards=(), held_as=jnp.bfloat16):
    loudness = steps_of(rng, extent, shards, -0.22, 0.18) if shards else 1.0
    values = jax.random.normal(rng, extent, jnp.float32) * spread * loudness
    return jnp.minimum(jnp.maximum(values, -reach), reach).astype(held_as)


def setup_inputs(seed: int = 0) -> dict:
    keys = jax.random.split(jax.random.key(seed), 5)
    return {
        "samples": gaussian(keys[0], (2, RANGE, RX, K), 1.0, 6.0, ((2, 4), (3, 8))),
        "tx_offsets": draw_tx_offsets(jax.random.fold_in(keys[4], 71), 0),
        "band_owner": draw_band_owner(jax.random.fold_in(keys[4], 71), 0),
        "beam_weights": gaussian(keys[3], (2, B, CHANNELS), (2 * CHANNELS) ** -0.5, 0.109375),
    }


def dft_pair(size):
    indices = jnp.arange(size, dtype=jnp.int32)
    product = indices[:, None] * indices[None, :] % size
    phase_angle = product.astype(jnp.float32) * (-2.0 * math.pi / size)
    scale = 1.0 / math.sqrt(size)
    return ((jnp.cos(phase_angle) * scale).astype(jnp.bfloat16), (jnp.sin(phase_angle) * scale).astype(jnp.bfloat16))

def twiddle_table():
    outer = jnp.arange(K1, dtype=jnp.int32)[:, None]
    inner = jnp.arange(K2, dtype=jnp.int32)[None, :]
    phase_angle = (outer * inner % (K1 * K2)).astype(jnp.float32) * (-2.0 * math.pi / (K1 * K2))
    return (jnp.cos(phase_angle), jnp.sin(phase_angle))

def phase_table():
    sender = jnp.arange(TX, dtype=jnp.int32)[:, None]
    speed = jnp.arange(V, dtype=jnp.int32)[None, :] - V // 2
    phase_angle = (sender * speed).astype(jnp.float32) * (-2.0 * math.pi / (TX * V))
    return (jnp.cos(phase_angle), jnp.sin(phase_angle))

def spectrum_of(real_part, imag_part, row_count):
    split_re = real_part.reshape(row_count, K1, K2).astype(jnp.float32)
    split_im = imag_part.reshape(row_count, K1, K2).astype(jnp.float32)
    table_re, table_im = dft_pair(K1)
    table_re = table_re.astype(jnp.float32)
    table_im = table_im.astype(jnp.float32)
    section_re = jnp.einsum('kn,rnm->rkm', table_re, split_re) - jnp.einsum('kn,rnm->rkm', table_im, split_im)
    section_im = jnp.einsum('kn,rnm->rkm', table_re, split_im) + jnp.einsum('kn,rnm->rkm', table_im, split_re)
    twist_re, twist_im = twiddle_table()
    turned_re = (section_re * twist_re - section_im * twist_im).astype(jnp.bfloat16).astype(jnp.float32)
    turned_im = (section_re * twist_im + section_im * twist_re).astype(jnp.bfloat16).astype(jnp.float32)
    final_re, final_im = dft_pair(K2)
    final_re = final_re.astype(jnp.float32)
    final_im = final_im.astype(jnp.float32)
    out_re = jnp.einsum('qm,rkm->rqk', final_re, turned_re) - jnp.einsum('qm,rkm->rqk', final_im, turned_im)
    out_im = jnp.einsum('qm,rkm->rqk', final_re, turned_im) + jnp.einsum('qm,rkm->rqk', final_im, turned_re)
    return (out_re.reshape(row_count, K1 * K2).astype(jnp.bfloat16), out_im.reshape(row_count, K1 * K2).astype(jnp.bfloat16))

def reference(samples, tx_offsets, band_owner, beam_weights):
    starts = ((tx_offsets - V // 2) % K).astype(jnp.int32)
    cos_part, sin_part = phase_table()
    cos_part = cos_part[:, None, :]
    sin_part = sin_part[:, None, :]
    weight_re = beam_weights[0]
    weight_im = beam_weights[1]

    def one_bin(position):
        cube = lax.dynamic_index_in_dim(samples, position, 1, keepdims=False)
        spec_re, spec_im = spectrum_of(cube[0], cube[1], RX)
        joined = jnp.stack([spec_re, spec_im])
        double = jnp.concatenate([joined, joined], axis=2)

        def take_band(begin_at):
            return lax.dynamic_slice_in_dim(double, begin_at, V, 2)
        picked = jax.vmap(take_band)(starts)
        got_re = picked[:, 0].astype(jnp.float32)
        got_im = picked[:, 1].astype(jnp.float32)
        demux_re = (got_re * cos_part - got_im * sin_part).astype(jnp.bfloat16).reshape(TX * RX, V)
        demux_im = (got_re * sin_part + got_im * cos_part).astype(jnp.bfloat16).reshape(TX * RX, V)
        beam_re = jnp.dot(weight_re, demux_re, preferred_element_type=jnp.float32) - jnp.dot(weight_im, demux_im, preferred_element_type=jnp.float32)
        beam_im = jnp.dot(weight_re, demux_im, preferred_element_type=jnp.float32) + jnp.dot(weight_im, demux_re, preferred_element_type=jnp.float32)
        return jnp.stack([beam_re, beam_im]).astype(jnp.bfloat16)
    beams = lax.map(one_bin, jnp.arange(RANGE, dtype=jnp.int32))
    tiles = beams.reshape(RANGE, 2, B, BANDS, BW).transpose(3, 1, 2, 0, 4).reshape(BANDS, 2, B, RANGE * BW)
    counter = jnp.arange(BANDS, dtype=jnp.int32)
    same_owner = band_owner[:, None] == band_owner[None, :]
    earlier = counter[None, :] < counter[:, None]
    band_rank = lax.optimization_barrier(jnp.sum((same_owner & earlier).astype(jnp.int32), axis=1)).astype(jnp.int32)
    slot_ids = (band_owner * CAP + band_rank).astype(jnp.int32)
    store = jnp.zeros((N_RX * CAP, 2, B, RANGE * BW), jnp.bfloat16)
    return store.at[slot_ids].set(tiles)
```

```python
from functools import partial
import math

import jax
import jax.numpy as jnp
from jax import lax
from jax.experimental import pallas as pl
from jax.experimental.pallas import tpu as pltpu
from jax.sharding import PartitionSpec as P

K1 = 64
K2 = 64
SLOTS = 16


def dft_pair(size):
    indices = jnp.arange(size, dtype=jnp.int32)
    product = indices[:, None] * indices[None, :] % size
    phase_angle = product.astype(jnp.float32) * (-2.0 * math.pi / size)
    scale = 1.0 / math.sqrt(size)
    return (
        (jnp.cos(phase_angle) * scale).astype(jnp.bfloat16),
        (jnp.sin(phase_angle) * scale).astype(jnp.bfloat16),
    )


def twiddle_table():
    outer = jnp.arange(K1, dtype=jnp.int32)[:, None]
    inner = jnp.arange(K2, dtype=jnp.int32)[None, :]
    phase_angle = (outer * inner % (K1 * K2)).astype(jnp.float32) * (-2.0 * math.pi / (K1 * K2))
    return (jnp.cos(phase_angle), jnp.sin(phase_angle))


def spectrum_of(real_part, imag_part, row_count):
    mixing = partial(jnp.einsum, preferred_element_type=jnp.float32)
    split_re = real_part.reshape(row_count, K1, K2)
    split_im = imag_part.reshape(row_count, K1, K2)
    table_re, table_im = dft_pair(K1)
    section_re = mixing("kn,rnm->rkm", table_re, split_re) - mixing(
        "kn,rnm->rkm", table_im, split_im
    )
    section_im = mixing("kn,rnm->rkm", table_re, split_im) + mixing(
        "kn,rnm->rkm", table_im, split_re
    )
    twist_re, twist_im = twiddle_table()
    turned_re = (section_re * twist_re - section_im * twist_im).astype(jnp.bfloat16)
    turned_im = (section_re * twist_im + section_im * twist_re).astype(jnp.bfloat16)
    final_re, final_im = dft_pair(K2)
    out_re = mixing("qm,rkm->rqk", final_re, turned_re) - mixing("qm,rkm->rqk", final_im, turned_im)
    out_im = mixing("qm,rkm->rqk", final_re, turned_im) + mixing("qm,rkm->rqk", final_im, turned_re)
    return (
        out_re.reshape(row_count, K1 * K2).astype(jnp.bfloat16),
        out_im.reshape(row_count, K1 * K2).astype(jnp.bfloat16),
    )


def general(samples, tx_offsets, band_owner, beam_weights):
    owners = lax.axis_size("rx")
    band_count = band_owner.shape[0]
    capacity = 3 * band_count // owners
    tx_count = tx_offsets.shape[0]
    bin_count = K1 * K2
    speed_bins = bin_count // SLOTS
    band_width = speed_bins // band_count
    starts = (tx_offsets - speed_bins // 2) % bin_count
    sender = jnp.arange(tx_count, dtype=jnp.int32)[:, None]
    speed = jnp.arange(speed_bins, dtype=jnp.int32)[None, :] - speed_bins // 2
    phase_angle = (sender * speed).astype(jnp.float32) * (-2.0 * math.pi / (tx_count * speed_bins))
    cos_part = jnp.cos(phase_angle)[:, None, None, :]
    sin_part = jnp.sin(phase_angle)[:, None, None, :]
    pieces = lax.all_to_all(samples, "chirp", split_axis=1, concat_axis=3, tiled=True)
    bin_rows = pieces.shape[1]
    item_count = pieces.shape[2]
    spec_re, spec_im = spectrum_of(
        pieces[0].reshape(bin_rows * item_count, bin_count),
        pieces[1].reshape(bin_rows * item_count, bin_count),
        bin_rows * item_count,
    )
    joined = jnp.stack([spec_re, spec_im]).reshape(2, bin_rows, item_count, bin_count)
    double = jnp.concatenate([joined, joined], axis=3)

    def take_band(begin_at):
        return lax.dynamic_slice_in_dim(double, begin_at, speed_bins, 3)

    picked = jax.vmap(take_band)(starts)
    got_re = picked[:, 0].astype(jnp.float32)
    got_im = picked[:, 1].astype(jnp.float32)
    demux_re = got_re * cos_part - got_im * sin_part
    demux_im = got_re * sin_part + got_im * cos_part
    demuxed = jnp.stack([demux_re, demux_im]).astype(jnp.bfloat16)
    demuxed = demuxed.transpose(0, 1, 3, 2, 4)
    rx_local = demuxed.shape[2]
    bin_rows = demuxed.shape[3]
    tile_width = bin_rows * band_width
    tiles = demuxed.reshape(2, tx_count, rx_local, bin_rows, band_count, band_width)
    tiles = tiles.transpose(4, 0, 1, 2, 3, 5).reshape(band_count, 2, tx_count, rx_local, tile_width)
    counter = jnp.arange(band_count, dtype=jnp.int32)
    same_owner = band_owner[:, None] == band_owner[None, :]
    earlier = counter[None, :] < counter[:, None]
    band_rank = jnp.sum((same_owner & earlier).astype(jnp.int32), axis=1)
    weight_re = beam_weights[0]
    weight_im = beam_weights[1]
    slot_ids = band_owner * capacity + band_rank
    choose = (slot_ids[None, :] == jnp.arange(owners * capacity, dtype=jnp.int32)[:, None]).astype(
        jnp.bfloat16
    )
    outgoing = jnp.dot(
        choose, tiles.reshape(band_count, -1), preferred_element_type=jnp.float32
    ).astype(jnp.bfloat16)
    outgoing = outgoing.reshape(owners, capacity, 2, tx_count, rx_local, tile_width)
    slots = lax.all_to_all(outgoing, "rx", split_axis=0, concat_axis=4, tiled=True)[0]
    item_count = slots.shape[0]
    channels = slots.reshape(item_count, 2, slots.shape[2] * slots.shape[3], slots.shape[4])
    mixing = partial(jnp.einsum, preferred_element_type=jnp.float32)
    beam_re = mixing("bc,scm->sbm", weight_re, channels[:, 0]) - mixing(
        "bc,scm->sbm", weight_im, channels[:, 1]
    )
    beam_im = mixing("bc,scm->sbm", weight_re, channels[:, 1]) + mixing(
        "bc,scm->sbm", weight_im, channels[:, 0]
    )
    return jnp.stack([beam_re, beam_im], axis=1).astype(jnp.bfloat16)


LANES = 128
GROUPS = 32


def fourier_of_8(re, im):
    half = math.sqrt(0.5)

    def fourier_of_4(a, b, c, d):
        s0, s1 = (a[0] + c[0], a[1] + c[1]), (a[0] - c[0], a[1] - c[1])
        s2, s3 = (b[0] + d[0], b[1] + d[1]), (b[0] - d[0], b[1] - d[1])
        return (
            (s0[0] + s2[0], s0[1] + s2[1]),
            (s1[0] + s3[1], s1[1] - s3[0]),
            (s0[0] - s2[0], s0[1] - s2[1]),
            (s1[0] - s3[1], s1[1] + s3[0]),
        )

    x = list(zip(re, im))
    even = fourier_of_4(x[0], x[2], x[4], x[6])
    odd = fourier_of_4(x[1], x[3], x[5], x[7])
    o1 = ((odd[1][0] + odd[1][1]) * half, (odd[1][1] - odd[1][0]) * half)
    o3 = ((odd[3][1] - odd[3][0]) * half, -(odd[3][0] + odd[3][1]) * half)
    turned = (odd[0], o1, (odd[2][1], -odd[2][0]), o3)
    first = [(e[0] + o[0], e[1] + o[1]) for e, o in zip(even, turned)]
    second = [(e[0] - o[0], e[1] - o[1]) for e, o in zip(even, turned)]
    return first + second


def beams_kernel(
    chunk_bins, rows, slot_ids, x_ref, table_ref, weight_ref, out_ref, part, mixed, spread, masked
):
    sources = x_ref.shape[0]
    folds = x_ref.shape[4] // LANES
    tx2 = spread.shape[0]
    halves = rows // 16

    def transform(step, carry):
        q = step // halves
        r0 = pl.multiple_of((step % halves) * 16, 16)
        for fold in range(folds):
            re = [
                x_ref[c, 0, q, pl.ds(r0, 16), fold * LANES : (fold + 1) * LANES].astype(jnp.float32)
                for c in range(sources)
            ]
            im = [
                x_ref[c, 1, q, pl.ds(r0, 16), fold * LANES : (fold + 1) * LANES].astype(jnp.float32)
                for c in range(sources)
            ]
            for k, (a, b) in enumerate(fourier_of_8(re, im)):
                angle = -2.0 * math.pi * fold * k / GROUPS
                if fold * k:
                    c, s = math.cos(angle), math.sin(angle)
                    a, b = a * c - b * s, a * s + b * c
                part[fold, k, 0] = a
                part[fold, k, 1] = b
        base = pl.multiple_of(q * rows + r0, 16)
        for k in range(sources):
            v = [(part[f, k, 0], part[f, k, 1]) for f in range(folds)]
            s0, s1 = (v[0][0] + v[2][0], v[0][1] + v[2][1]), (v[0][0] - v[2][0], v[0][1] - v[2][1])
            s2, s3 = (v[1][0] + v[3][0], v[1][1] + v[3][1]), (v[1][0] - v[3][0], v[1][1] - v[3][1])
            outs = (
                (s0[0] + s2[0], s0[1] + s2[1]),
                (s1[0] + s3[1], s1[1] - s3[0]),
                (s0[0] - s2[0], s0[1] - s2[1]),
                (s1[0] - s3[1], s1[1] + s3[0]),
            )
            for f, (a, b) in enumerate(outs):
                mixed[k + sources * f, pl.ds(base, 16), :LANES] = a.astype(jnp.bfloat16)
                mixed[k + sources * f, pl.ds(base, 16), LANES:] = b.astype(jnp.bfloat16)
        return carry

    lax.fori_loop(0, chunk_bins * halves, transform, 0)

    def demultiplex(group, carry):
        got = lax.dot_general(
            table_ref[group], mixed[group], (((1,), (1,)), ((), ())),
            preferred_element_type=jnp.float32,
        )
        for t in range(tx2):
            spread[t, pl.ds(group, 8, stride=GROUPS), :] = got[8 * t : 8 * t + 8]
        return carry

    lax.fori_loop(0, GROUPS, demultiplex, 0, unroll=4)

    lane_bin = lax.broadcasted_iota(jnp.int32, (16, LANES), 1) // rows
    for t in range(tx2):
        def scatter(band, carry):
            at = pl.multiple_of(band * 16, 16)
            tile = spread[t, pl.ds(at, 16), :]
            for q in range(chunk_bins):
                kept = jnp.where(lane_bin == q, tile, 0.0).astype(jnp.bfloat16)
                to = pl.multiple_of((band * chunk_bins + q) * 16, 16)
                masked[pl.ds(to, 16), t * LANES : (t + 1) * LANES] = kept
            return carry

        lax.fori_loop(0, 16, scatter, 0, unroll=4)

    low = lax.broadcasted_iota(jnp.int32, (256, LANES), 1) < LANES // 2

    def combine(block, carry):
        at = pl.multiple_of(block * 256, 256)
        beams = lax.dot_general(
            weight_ref[...], masked[pl.ds(at, 256), :], (((1,), (1,)), ((), ())),
            preferred_element_type=jnp.float32,
        )
        for pair in range(2):
            top = beams[:256, pair * LANES : (pair + 1) * LANES]
            bottom = beams[256:, pair * LANES : (pair + 1) * LANES]
            even = jnp.where(low, top, pltpu.roll(bottom, LANES // 2, 1))
            odd = jnp.where(low, pltpu.roll(top, LANES // 2, 1), bottom)
            out_ref[slot_ids[4 * block + 2 * pair]] = even.astype(jnp.bfloat16)
            out_ref[slot_ids[4 * block + 2 * pair + 1]] = odd.astype(jnp.bfloat16)
        return carry

    lax.fori_loop(0, 4, combine, 0)


def beams_of(slot_ids, chunk, table, weights, slots):
    sources, _, chunk_bins, rows, _ = chunk.shape
    tx2 = table.shape[1] // 8
    vmem = pl.BlockSpec(memory_space=pltpu.VMEM)
    return pl.pallas_call(
        partial(beams_kernel, chunk_bins, rows),
        out_shape=jax.ShapeDtypeStruct((slots, 256, LANES), jnp.bfloat16),
        in_specs=[pl.BlockSpec(memory_space=pltpu.SMEM), vmem, vmem, vmem],
        out_specs=vmem,
        scratch_shapes=[
            pltpu.VMEM((4, 8, 2, 16, LANES), jnp.float32),
            pltpu.VMEM((GROUPS, LANES, 2 * LANES), jnp.bfloat16),
            pltpu.VMEM((tx2, 256, LANES), jnp.float32),
            pltpu.VMEM((1024, tx2 * LANES), jnp.bfloat16),
        ],
        compiler_params=pltpu.CompilerParams(vmem_limit_bytes=56 << 20),
        name="beams",
    )(slot_ids, chunk, table, weights)


def store_kernel(taken, *refs):
    *pieces, out_ref = refs
    slot = pl.program_id(0)
    used = slot < taken[0]
    low = lax.broadcasted_iota(jnp.int32, (256, LANES), 1) < LANES // 2
    sums = []
    for side in range(2):
        group = pieces[4 * side : 4 * side + 4]
        total = group[0][...].reshape(256, LANES).astype(jnp.float32)
        for ref in group[1:]:
            total = total + ref[...].reshape(256, LANES).astype(jnp.float32)
        sums.append(jnp.where(used, total, 0.0))
    first = jnp.where(low, sums[0], pltpu.roll(sums[1], LANES // 2, 1)).astype(jnp.bfloat16)
    second = jnp.where(low, pltpu.roll(sums[0], LANES // 2, 1), sums[1]).astype(jnp.bfloat16)
    out_ref[0, 0, :128, :] = first[:128]
    out_ref[0, 1, :128, :] = first[128:]
    out_ref[0, 0, 128:, :] = second[:128]
    out_ref[0, 1, 128:, :] = second[128:]


def store_pair(taken, me, left, right, so_far, pair, capacity):
    own = pl.BlockSpec((1, 1, 256, LANES), lambda s, taken, me: (me[0], s, 0, 0))
    got = pl.BlockSpec((1, 256, LANES), lambda s, taken, me: (s, 0, 0))
    specs = ([own] + [got] * 3) * 2
    args = [*left, *right]
    aliases = {}
    if so_far is not None:
        specs.append(pl.BlockSpec(memory_space=pl.ANY))
        args.append(so_far)
        aliases = {2 + 8: 0}

    def body(taken, me, *refs):
        store_kernel(taken, *refs[:8], refs[-1])

    return pl.pallas_call(
        body,
        out_shape=jax.ShapeDtypeStruct((capacity, 2, 256, 2 * LANES), jnp.bfloat16),
        grid_spec=pltpu.PrefetchScalarGridSpec(
            num_scalar_prefetch=2,
            grid=(capacity,),
            in_specs=specs,
            out_specs=pl.BlockSpec((1, 2, 256, LANES), lambda s, taken, me: (s, 0, 0, pair)),
        ),
        input_output_aliases=aliases,
        name="store",
    )(taken, me, *args)


def tuned(samples, tx_offsets, band_owner, beam_weights):
    owners = lax.axis_size("rx")
    spans = lax.axis_size("chirp")
    me = lax.axis_index("rx")
    bands = band_owner.shape[0]
    tx_count = tx_offsets.shape[0]
    capacity = 3 * bands // owners
    rows = samples.shape[2]
    bins = samples.shape[1] // spans
    chunk_bins = LANES // rows
    chunks = bins // chunk_bins
    slots = owners * capacity

    counter = jnp.arange(bands, dtype=jnp.int32)
    same_owner = band_owner[:, None] == band_owner[None, :]
    earlier = counter[None, :] < counter[:, None]
    band_rank = jnp.sum((same_owner & earlier).astype(jnp.int32), axis=1)
    slot_ids = band_owner * capacity + band_rank
    taken = jnp.sum((band_owner == me).astype(jnp.int32)).reshape(1)

    split = samples.reshape(2, spans, chunks, chunk_bins, rows, samples.shape[3])
    chunk_in = [split[:, :, i].transpose(1, 0, 2, 3, 4) for i in range(chunks)]

    two_pi = 2.0 * math.pi
    group = jnp.arange(GROUPS, dtype=jnp.int32)
    high = jnp.arange(8, dtype=jnp.int32)
    lane = jnp.arange(LANES, dtype=jnp.int32)
    sender = jnp.arange(tx_count, dtype=jnp.int32)
    start = tx_offsets[:, None] + 32 * high[None, :] + 4096 - 128
    a1 = (start[:, :, None] * lane % 4096).astype(jnp.float32) * (-two_pi / 4096)
    a2 = (group[:, None] * lane[None, :]).astype(jnp.float32) * (-two_pi / 4096)
    speed = 32 * high[None, :] + group[:, None] - 128
    a3 = (sender[None, :, None] * speed[:, None, :]).astype(jnp.float32) * (
        -two_pi / (tx_count * 256)
    )
    c1, s1 = lax.optimization_barrier((jnp.cos(a1), jnp.sin(a1)))
    c2, s2 = lax.optimization_barrier((jnp.cos(a2) / 64, jnp.sin(a2) / 64))
    c3, s3 = lax.optimization_barrier((jnp.cos(a3), jnp.sin(a3)))
    c2, s2 = c2[:, None, None, :], s2[:, None, None, :]
    c3, s3 = c3[..., None], s3[..., None]
    c12, s12 = c1 * c2 - s1 * s2, c1 * s2 + s1 * c2
    turn_re = (c12 * c3 - s12 * s3).reshape(GROUPS, tx_count * 8, LANES)
    turn_im = (c12 * s3 + s12 * c3).reshape(GROUPS, tx_count * 8, LANES)
    table = jnp.concatenate(
        [
            jnp.concatenate([turn_re, -turn_im], axis=2),
            jnp.concatenate([turn_im, turn_re], axis=2),
        ],
        axis=1,
    ).astype(jnp.bfloat16)

    local = lax.dynamic_slice_in_dim(
        beam_weights.reshape(2, 2, 128, tx_count, owners * rows), me * rows, rows, 4
    )
    local = jnp.tile(local, (1, 1, 1, 1, chunk_bins))
    local = local.reshape(2, 2, 128, tx_count * LANES)
    weights = jnp.stack(
        [
            jnp.concatenate([local[0], -local[1]], axis=2),
            jnp.concatenate([local[1], local[0]], axis=2),
        ],
        axis=1,
    ).reshape(512, 2 * tx_count * LANES)

    swaps = [[(i, i ^ k) for i in range(owners)] for k in range(owners)]
    shares = [None] * chunks
    arrived = [None] * chunks
    for i in range(chunks):
        piece = chunk_in[i]
        if i >= 2:
            piece, shares[i - 2] = lax.optimization_barrier((piece, shares[i - 2]))
        arrived[i] = lax.all_to_all(piece, "chirp", split_axis=0, concat_axis=0, tiled=True)
        if i >= 1:
            shares[i - 1] = beams_of(slot_ids, arrived[i - 1], table, weights, slots)
    shares[-1] = beams_of(slot_ids, arrived[-1], table, weights, slots)

    groups = []
    for i in range(chunks):
        whole = shares[i].reshape(owners, capacity, 256, LANES)
        got = [
            lax.ppermute(lax.dynamic_index_in_dim(whole, me ^ k, 0, keepdims=False), "rx", swaps[k])
            for k in range(1, owners)
        ]
        groups.append([whole] + got)
    store = None
    for pair in range(chunks // 2):
        store = store_pair(
            taken, me.reshape(1), groups[2 * pair], groups[2 * pair + 1], store, pair, capacity
        )
    return store


def shards(samples, tx_offsets, band_owner, beam_weights):
    fits = (
        lax.axis_size("rx") == 4
        and lax.axis_size("chirp") == 8
        and samples.shape == (2, 128, 32, 512)
        and beam_weights.shape == (2, 256, 1536)
    )
    return (tuned if fits else general)(samples, tx_offsets, band_owner, beam_weights)


def solution(mesh):
    placed = (P(None, None, "rx", "chirp"), P(), P(), P())
    return jax.shard_map(
        shards, mesh=mesh, in_specs=placed, out_specs=P("rx", None, None, "chirp"), check_vma=False
    )
```

```python
from functools import partial
import math

import jax
import jax.numpy as jnp
from jax import lax
from jax.experimental import pallas as pl
from jax.experimental.pallas import tpu as pltpu
from jax.sharding import PartitionSpec as P

K1 = 64
K2 = 64
SLOTS = 16


def dft_pair(size):
    indices = jnp.arange(size, dtype=jnp.int32)
    product = indices[:, None] * indices[None, :] % size
    phase_angle = product.astype(jnp.float32) * (-2.0 * math.pi / size)
    scale = 1.0 / math.sqrt(size)
    return (
        (jnp.cos(phase_angle) * scale).astype(jnp.bfloat16),
        (jnp.sin(phase_angle) * scale).astype(jnp.bfloat16),
    )


def twiddle_table():
    outer = jnp.arange(K1, dtype=jnp.int32)[:, None]
    inner = jnp.arange(K2, dtype=jnp.int32)[None, :]
    phase_angle = (outer * inner % (K1 * K2)).astype(jnp.float32) * (-2.0 * math.pi / (K1 * K2))
    return (jnp.cos(phase_angle), jnp.sin(phase_angle))


def spectrum_of(real_part, imag_part, row_count):
    mixing = partial(jnp.einsum, preferred_element_type=jnp.float32)
    split_re = real_part.reshape(row_count, K1, K2)
    split_im = imag_part.reshape(row_count, K1, K2)
    table_re, table_im = dft_pair(K1)
    section_re = mixing("kn,rnm->rkm", table_re, split_re) - mixing(
        "kn,rnm->rkm", table_im, split_im
    )
    section_im = mixing("kn,rnm->rkm", table_re, split_im) + mixing(
        "kn,rnm->rkm", table_im, split_re
    )
    twist_re, twist_im = twiddle_table()
    turned_re = (section_re * twist_re - section_im * twist_im).astype(jnp.bfloat16)
    turned_im = (section_re * twist_im + section_im * twist_re).astype(jnp.bfloat16)
    final_re, final_im = dft_pair(K2)
    out_re = mixing("qm,rkm->rqk", final_re, turned_re) - mixing("qm,rkm->rqk", final_im, turned_im)
    out_im = mixing("qm,rkm->rqk", final_re, turned_im) + mixing("qm,rkm->rqk", final_im, turned_re)
    return (
        out_re.reshape(row_count, K1 * K2).astype(jnp.bfloat16),
        out_im.reshape(row_count, K1 * K2).astype(jnp.bfloat16),
    )


def general(samples, tx_offsets, band_owner, beam_weights):
    owners = lax.axis_size("rx")
    band_count = band_owner.shape[0]
    capacity = 3 * band_count // owners
    tx_count = tx_offsets.shape[0]
    bin_count = K1 * K2
    speed_bins = bin_count // SLOTS
    band_width = speed_bins // band_count
    starts = (tx_offsets - speed_bins // 2) % bin_count
    sender = jnp.arange(tx_count, dtype=jnp.int32)[:, None]
    speed = jnp.arange(speed_bins, dtype=jnp.int32)[None, :] - speed_bins // 2
    phase_angle = (sender * speed).astype(jnp.float32) * (-2.0 * math.pi / (tx_count * speed_bins))
    cos_part = jnp.cos(phase_angle)[:, None, None, :]
    sin_part = jnp.sin(phase_angle)[:, None, None, :]
    pieces = lax.all_to_all(samples, "chirp", split_axis=1, concat_axis=3, tiled=True)
    bin_rows = pieces.shape[1]
    item_count = pieces.shape[2]
    spec_re, spec_im = spectrum_of(
        pieces[0].reshape(bin_rows * item_count, bin_count),
        pieces[1].reshape(bin_rows * item_count, bin_count),
        bin_rows * item_count,
    )
    joined = jnp.stack([spec_re, spec_im]).reshape(2, bin_rows, item_count, bin_count)
    double = jnp.concatenate([joined, joined], axis=3)

    def take_band(begin_at):
        return lax.dynamic_slice_in_dim(double, begin_at, speed_bins, 3)

    picked = jax.vmap(take_band)(starts)
    got_re = picked[:, 0].astype(jnp.float32)
    got_im = picked[:, 1].astype(jnp.float32)
    demux_re = got_re * cos_part - got_im * sin_part
    demux_im = got_re * sin_part + got_im * cos_part
    demuxed = jnp.stack([demux_re, demux_im]).astype(jnp.bfloat16)
    demuxed = demuxed.transpose(0, 1, 3, 2, 4)
    rx_local = demuxed.shape[2]
    bin_rows = demuxed.shape[3]
    tile_width = bin_rows * band_width
    tiles = demuxed.reshape(2, tx_count, rx_local, bin_rows, band_count, band_width)
    tiles = tiles.transpose(4, 0, 1, 2, 3, 5).reshape(band_count, 2, tx_count, rx_local, tile_width)
    counter = jnp.arange(band_count, dtype=jnp.int32)
    same_owner = band_owner[:, None] == band_owner[None, :]
    earlier = counter[None, :] < counter[:, None]
    band_rank = jnp.sum((same_owner & earlier).astype(jnp.int32), axis=1)
    weight_re = beam_weights[0]
    weight_im = beam_weights[1]
    slot_ids = band_owner * capacity + band_rank
    choose = (slot_ids[None, :] == jnp.arange(owners * capacity, dtype=jnp.int32)[:, None]).astype(
        jnp.bfloat16
    )
    outgoing = jnp.dot(
        choose, tiles.reshape(band_count, -1), preferred_element_type=jnp.float32
    ).astype(jnp.bfloat16)
    outgoing = outgoing.reshape(owners, capacity, 2, tx_count, rx_local, tile_width)
    slots = lax.all_to_all(outgoing, "rx", split_axis=0, concat_axis=4, tiled=True)[0]
    item_count = slots.shape[0]
    channels = slots.reshape(item_count, 2, slots.shape[2] * slots.shape[3], slots.shape[4])
    mixing = partial(jnp.einsum, preferred_element_type=jnp.float32)
    beam_re = mixing("bc,scm->sbm", weight_re, channels[:, 0]) - mixing(
        "bc,scm->sbm", weight_im, channels[:, 1]
    )
    beam_im = mixing("bc,scm->sbm", weight_re, channels[:, 1]) + mixing(
        "bc,scm->sbm", weight_im, channels[:, 0]
    )
    return jnp.stack([beam_re, beam_im], axis=1).astype(jnp.bfloat16)


LANES = 128
GROUPS = 32


def fourier_of_8(re, im):
    half = math.sqrt(0.5)

    x = list(zip(re, im))
    even = fourier_of_4(x[0], x[2], x[4], x[6])
    odd = fourier_of_4(x[1], x[3], x[5], x[7])
    o1 = ((odd[1][0] + odd[1][1]) * half, (odd[1][1] - odd[1][0]) * half)
    o3 = ((odd[3][1] - odd[3][0]) * half, -(odd[3][0] + odd[3][1]) * half)
    turned = (odd[0], o1, (odd[2][1], -odd[2][0]), o3)
    first = [(e[0] + o[0], e[1] + o[1]) for e, o in zip(even, turned)]
    second = [(e[0] - o[0], e[1] - o[1]) for e, o in zip(even, turned)]
    return first + second


def swap_lanes(tiles):
    tiles = list(tiles)
    lane = lax.broadcasted_iota(jnp.int32, tiles[0].shape, 1)
    width = LANES // 2
    step = len(tiles) // 2
    while step:
        keep = lane // width % 2 == 0
        for i in range(len(tiles)):
            if i // step % 2 == 0:
                a, b = tiles[i], tiles[i + step]
                tiles[i] = jnp.where(keep, a, pltpu.roll(b, width, 1))
                tiles[i + step] = jnp.where(keep, pltpu.roll(a, LANES - width, 1), b)
        width //= 2
        step //= 2
    return tiles


def fourier_of_4(a, b, c, d):
    s0, s1 = (a[0] + c[0], a[1] + c[1]), (a[0] - c[0], a[1] - c[1])
    s2, s3 = (b[0] + d[0], b[1] + d[1]), (b[0] - d[0], b[1] - d[1])
    return (
        (s0[0] + s2[0], s0[1] + s2[1]),
        (s1[0] + s3[1], s1[1] - s3[0]),
        (s0[0] - s2[0], s0[1] - s2[1]),
        (s1[0] - s3[1], s1[1] + s3[0]),
    )


def beams_kernel(owners, sources, near, far, first, samples_ref, *refs):
    pieces = refs[: sources - 1]
    table_hbm, weight_hbm = refs[sources - 1 : sources + 1]
    outs = refs[sources + 1 : sources + 1 + owners]
    x, table, weight, part, mixed, spread, packed, staged, x_sem, in_sem, out_sem = refs[
        sources + 1 + owners :
    ]
    chunk_bins, rows = x.shape[2], x.shape[3]
    folds = x.shape[4] // LANES
    tx2 = spread.shape[0]
    halves = rows // 16

    own = samples_ref.at[:, pl.ds(first[0], chunk_bins)]
    here = first[1]
    loads = [pltpu.make_async_copy(own, x.at[here], x_sem.at[0])]
    for c in range(1, sources):
        loads.append(pltpu.make_async_copy(pieces[c - 1], x.at[here ^ c], x_sem.at[c]))
    load_table = pltpu.make_async_copy(table_hbm, table, in_sem.at[0])
    load_weight = pltpu.make_async_copy(weight_hbm, weight, in_sem.at[1])
    for load in loads:
        load.start()
    load_table.start()
    load_weight.start()
    for load in loads:
        load.wait()

    def transform(step, carry):
        q = step // halves
        r0 = pl.multiple_of((step % halves) * 16, 16)
        for fold in range(folds):
            span = slice(fold * LANES, (fold + 1) * LANES)
            re = [x[c, 0, q, pl.ds(r0, 16), span].astype(jnp.float32) for c in range(sources)]
            im = [x[c, 1, q, pl.ds(r0, 16), span].astype(jnp.float32) for c in range(sources)]
            for k, (a, b) in enumerate(fourier_of_8(re, im)):
                if fold * k:
                    angle = -2.0 * math.pi * fold * k / GROUPS
                    c, s = math.cos(angle), math.sin(angle)
                    a, b = a * c - b * s, a * s + b * c
                part[fold, k, 0] = a
                part[fold, k, 1] = b
        base = pl.multiple_of(q * rows + r0, 16)
        for k in range(sources):
            quarter = fourier_of_4(*((part[f, k, 0], part[f, k, 1]) for f in range(folds)))
            for f, (a, b) in enumerate(quarter):
                mixed[k + sources * f, pl.ds(base, 16), :LANES] = a.astype(jnp.bfloat16)
                mixed[k + sources * f, pl.ds(base, 16), LANES:] = b.astype(jnp.bfloat16)
        return carry

    lax.fori_loop(0, chunk_bins * halves, transform, 0)
    load_table.wait()

    def demultiplex(group, carry):
        got = lax.dot_general(
            table[group], mixed[group], (((1,), (1,)), ((), ())),
            preferred_element_type=jnp.float32,
        )
        for t in range(tx2):
            spread[t, pl.ds(group, 8, stride=GROUPS), :] = got[8 * t : 8 * t + 8]
        return carry

    lax.fori_loop(0, GROUPS, demultiplex, 0, unroll=16)

    def regroup(band, carry):
        at = pl.multiple_of(band * 16, 16)
        for t in range(tx2 // 4):
            tiles = swap_lanes([spread[4 * t + i, pl.ds(at, 16), :] for i in range(4)])
            for q in range(chunk_bins):
                to = pl.multiple_of((band * chunk_bins + q) * 16, 16)
                packed[pl.ds(to, 16), t * LANES : (t + 1) * LANES] = tiles[q].astype(jnp.bfloat16)
        return carry

    lax.fori_loop(0, 16, regroup, 0, unroll=2)
    load_weight.wait()

    def send(band):
        for k in range(owners):
            @pl.when(near[band] == k)
            def _():
                pltpu.make_async_copy(
                    staged.at[band], outs[k].at[far[band]], out_sem.at[band]
                ).start()

    parts = LANES // 16 // chunk_bins
    height = 512 // parts
    for block in range(chunk_bins):
        beams = lax.dot_general(
            weight[...], packed[256 * block : 256 * block + 256], (((1,), (1,)), ((), ())),
            preferred_element_type=jnp.float32,
        )
        for pair in range(2):
            lanes = slice(pair * LANES, (pair + 1) * LANES)
            tiles = swap_lanes(
                [beams[height * p : height * p + height, lanes] for p in range(parts)]
            )
            for side in range(parts):
                band = (2 * block + pair) * parts + side
                staged[band] = tiles[side].astype(jnp.bfloat16)
                send(band)
    for band in range(16):
        pltpu.make_async_copy(staged.at[band], outs[0].at[0], out_sem.at[band]).wait()


def beams_of(near, far, first, samples, pieces, table, weights, owners, capacity):
    sources = len(pieces) + 1
    piece = pieces[0].shape
    share = (512 * 16 * piece[1] // LANES, LANES)
    tx2 = table.shape[1] // 8
    smem = pl.BlockSpec(memory_space=pltpu.SMEM)
    hbm = pl.BlockSpec(memory_space=pl.ANY)
    return pl.pallas_call(
        partial(beams_kernel, owners, sources),
        out_shape=[jax.ShapeDtypeStruct((capacity, *share), jnp.bfloat16)] * owners,
        in_specs=[smem] * 3 + [hbm] * (sources + 2),
        out_specs=[hbm] * owners,
        scratch_shapes=[
            pltpu.VMEM((sources,) + piece, jnp.bfloat16),
            pltpu.VMEM(table.shape, jnp.bfloat16),
            pltpu.VMEM(weights.shape, jnp.bfloat16),
            pltpu.VMEM((4, 8, 2, 16, LANES), jnp.float32),
            pltpu.VMEM((GROUPS, LANES, 2 * LANES), jnp.bfloat16),
            pltpu.VMEM((tx2, 256, LANES), jnp.float32),
            pltpu.VMEM((256 * piece[1], tx2 // 4 * LANES), jnp.bfloat16),
            pltpu.VMEM((16, *share), jnp.bfloat16),
            pltpu.SemaphoreType.DMA((sources,)),
            pltpu.SemaphoreType.DMA((2,)),
            pltpu.SemaphoreType.DMA((16,)),
        ],
        compiler_params=pltpu.CompilerParams(vmem_limit_bytes=40 << 20),
        name="beams",
    )(near, far, first, samples, *pieces, table, weights)


STORE_SLOTS = 3
AFTER = ((), ((0, 3),), ((0, 4), (0, 7)), ((1, 4), (1, 7)), ((2, 4), (3, 4), (3, 7)))
ORDER = (4, 5, 6, 7, 2, 3, 1)


def store_kernel(owners, taken, *refs):
    *shares, out_ref = refs
    lane = lax.broadcasted_iota(jnp.int32, (128, LANES), 1)
    for s in range(STORE_SLOTS):
        used = pl.program_id(0) * STORE_SLOTS + s < taken[0]
        sums = []
        for c in range(0, len(shares), owners):
            total = shares[c][s].astype(jnp.float32)
            for ref in shares[c + 1 : c + owners]:
                total = total + ref[s].astype(jnp.float32)
            sums.append(jnp.where(used, total, 0.0))
        for quarter in range(4):
            tile, start = None, 0
            for total in sums:
                per_part = total.shape[0] // 128
                part, inner = quarter // per_part, quarter % per_part
                width = 32 * per_part
                piece = total[128 * inner : 128 * inner + 128]
                shift = (start - part * width) % LANES
                piece = pltpu.roll(piece, shift, 1) if shift else piece
                tile = piece if tile is None else jnp.where(lane < start, tile, piece)
                start += width
            tile = tile.astype(jnp.bfloat16)
            out_ref[s, 0, 64 * quarter : 64 * quarter + 64, :] = tile[:64]
            out_ref[s, 1, 64 * quarter : 64 * quarter + 64, :] = tile[64:]


def store_tile(taken, chunks, so_far, tile, capacity):
    owners = len(chunks[0])
    args = [share for chunk in chunks for share in chunk]
    specs = [pl.BlockSpec((STORE_SLOTS,) + a.shape[1:], lambda s, taken: (s, 0, 0)) for a in args]
    count = len(args)
    aliases = {}
    if so_far is not None:
        specs.append(pl.BlockSpec(memory_space=pl.ANY))
        args.append(so_far)
        aliases = {1 + count: 0}

    def body(taken, *refs):
        store_kernel(owners, taken, *refs[:count], refs[-1])

    return pl.pallas_call(
        body,
        out_shape=jax.ShapeDtypeStruct((capacity, 2, 256, 2 * LANES), jnp.bfloat16),
        grid_spec=pltpu.PrefetchScalarGridSpec(
            num_scalar_prefetch=1,
            grid=(capacity // STORE_SLOTS,),
            in_specs=specs,
            out_specs=pl.BlockSpec((STORE_SLOTS, 2, 256, LANES), lambda s, taken: (s, 0, 0, tile)),
        ),
        input_output_aliases=aliases,
        name="store",
    )(taken, *args)


def tuned(samples, tx_offsets, band_owner, beam_weights):
    owners = lax.axis_size("rx")
    spans = lax.axis_size("chirp")
    me = lax.axis_index("rx")
    bands = band_owner.shape[0]
    tx_count = tx_offsets.shape[0]
    capacity = 3 * bands // owners
    rows = samples.shape[2]
    bins = samples.shape[1] // spans

    counter = jnp.arange(bands, dtype=jnp.int32)
    same_owner = band_owner[:, None] == band_owner[None, :]
    earlier = counter[None, :] < counter[:, None]
    band_rank = jnp.sum((same_owner & earlier).astype(jnp.int32), axis=1)
    near = band_owner ^ me
    taken = jnp.sum((band_owner == me).astype(jnp.int32)).reshape(1)

    here = lax.axis_index("chirp")
    two_pi = 2.0 * math.pi
    group = jnp.arange(GROUPS, dtype=jnp.int32)
    high = jnp.arange(8, dtype=jnp.int32)
    lane = jnp.arange(LANES, dtype=jnp.int32)
    sender = jnp.arange(tx_count, dtype=jnp.int32)
    start = tx_offsets[:, None] + 32 * high[None, :] + 4096 - 128
    a1 = (start[:, :, None] * lane % 4096).astype(jnp.float32) * (-two_pi / 4096)
    a2 = (group[:, None] * lane[None, :]).astype(jnp.float32) * (-two_pi / 4096)
    speed = 32 * high[None, :] + group[:, None] - 128
    a3 = (sender[None, :, None] * speed[:, None, :]).astype(jnp.float32) * (
        -two_pi / (tx_count * 256)
    )
    c1, s1 = lax.optimization_barrier((jnp.cos(a1), jnp.sin(a1)))
    c2, s2 = lax.optimization_barrier((jnp.cos(a2) / 64, jnp.sin(a2) / 64))
    c3, s3 = lax.optimization_barrier((jnp.cos(a3), jnp.sin(a3)))
    c2, s2 = c2[:, None, None, :], s2[:, None, None, :]
    c3, s3 = c3[..., None], s3[..., None]
    c12, s12 = c1 * c2 - s1 * s2, c1 * s2 + s1 * c2
    turn_re = (c12 * c3 - s12 * s3).reshape(GROUPS, tx_count * 8, LANES)
    turn_im = (c12 * s3 + s12 * c3).reshape(GROUPS, tx_count * 8, LANES)
    table = jnp.concatenate(
        [
            jnp.concatenate([turn_re, -turn_im], axis=2),
            jnp.concatenate([turn_im, turn_re], axis=2),
        ],
        axis=1,
    ).astype(jnp.bfloat16)

    local = lax.dynamic_slice_in_dim(
        beam_weights.reshape(2, 4, 64, tx_count, owners * rows), me * rows, rows, 4
    )
    local = local.reshape(2, 4, 64, tx_count * rows)
    weights = jnp.stack(
        [
            jnp.concatenate([local[0], -local[1]], axis=2),
            jnp.concatenate([local[1], local[0]], axis=2),
        ],
        axis=1,
    ).reshape(512, 2 * tx_count * rows)

    crossings = [[(i, i ^ k) for i in range(spans)] for k in range(spans)]
    swaps = [[(i, i ^ k) for i in range(owners)] for k in range(owners)]
    plan = ((4, 4), (8, 4), (12, 4), (0, 2), (2, 2))
    shares, arrived = [], []

    def beams(i):
        at = jnp.stack([here * bins + plan[i][0], here]).astype(jnp.int32)
        shares.append(
            beams_of(near, band_rank, at, samples, arrived[i], table, weights, owners, capacity)
        )

    for i, (offset, count) in enumerate(plan):
        blocks = [
            lax.dynamic_slice_in_dim(samples, (here ^ k) * bins + offset, count, 1)
            for k in range(1, spans)
        ]
        after = [arrived[j][k - 1][0, 0, 0, :LANES] for j, k in AFTER[i]]
        if after:
            blocks, _ = lax.optimization_barrier((blocks, after))
        got = {k: lax.ppermute(blocks[k - 1], "chirp", crossings[k]) for k in ORDER}
        arrived.append([got[k] for k in range(1, spans)])
        if i:
            beams(i - 1)
    beams(len(plan) - 1)

    groups = []
    for share in shares:
        got = {k: lax.ppermute(share[k], "rx", swaps[k]) for k in reversed(range(1, owners))}
        groups.append([share[0]] + [got[k] for k in range(1, owners)])
    store = store_tile(taken, [groups[1], groups[2]], None, 1, capacity)
    return store_tile(taken, [groups[3], groups[4], groups[0]], store, 0, capacity)


def shards(samples, tx_offsets, band_owner, beam_weights):
    fits = (
        lax.axis_size("rx") == 4
        and lax.axis_size("chirp") == 8
        and samples.shape == (2, 128, 32, 512)
        and beam_weights.shape == (2, 256, 1536)
    )
    return (tuned if fits else general)(samples, tx_offsets, band_owner, beam_weights)


def solution(mesh):
    placed = (P(None, None, "rx", "chirp"), P(), P(), P())
    return jax.shard_map(
        shards, mesh=mesh, in_specs=placed, out_specs=P("rx", None, None, "chirp"), check_vma=False
    )
```

```python
from functools import partial
import math

import jax
import jax.numpy as jnp
from jax import lax
from jax.experimental import pallas as pl
from jax.experimental.pallas import tpu as pltpu
from jax.sharding import PartitionSpec as P


K1 = 64
K2 = 64
SLOTS = 16


def dft_pair(size):
    indices = jnp.arange(size, dtype=jnp.int32)
    product = indices[:, None] * indices[None, :] % size
    phase_angle = product.astype(jnp.float32) * (-2.0 * math.pi / size)
    scale = 1.0 / math.sqrt(size)
    return (
        (jnp.cos(phase_angle) * scale).astype(jnp.bfloat16),
        (jnp.sin(phase_angle) * scale).astype(jnp.bfloat16),
    )


def twiddle_table():
    outer = jnp.arange(K1, dtype=jnp.int32)[:, None]
    inner = jnp.arange(K2, dtype=jnp.int32)[None, :]
    phase_angle = (outer * inner % (K1 * K2)).astype(jnp.float32) * (-2.0 * math.pi / (K1 * K2))
    return (jnp.cos(phase_angle), jnp.sin(phase_angle))


def spectrum_of(real_part, imag_part, row_count):
    mixing = partial(jnp.einsum, preferred_element_type=jnp.float32)
    split_re = real_part.reshape(row_count, K1, K2)
    split_im = imag_part.reshape(row_count, K1, K2)
    table_re, table_im = dft_pair(K1)
    section_re = mixing("kn,rnm->rkm", table_re, split_re) - mixing(
        "kn,rnm->rkm", table_im, split_im
    )
    section_im = mixing("kn,rnm->rkm", table_re, split_im) + mixing(
        "kn,rnm->rkm", table_im, split_re
    )
    twist_re, twist_im = twiddle_table()
    turned_re = (section_re * twist_re - section_im * twist_im).astype(jnp.bfloat16)
    turned_im = (section_re * twist_im + section_im * twist_re).astype(jnp.bfloat16)
    final_re, final_im = dft_pair(K2)
    out_re = mixing("qm,rkm->rqk", final_re, turned_re) - mixing("qm,rkm->rqk", final_im, turned_im)
    out_im = mixing("qm,rkm->rqk", final_re, turned_im) + mixing("qm,rkm->rqk", final_im, turned_re)
    return (
        out_re.reshape(row_count, K1 * K2).astype(jnp.bfloat16),
        out_im.reshape(row_count, K1 * K2).astype(jnp.bfloat16),
    )


def general(samples, tx_offsets, band_owner, beam_weights):
    owners = lax.axis_size("rx")
    band_count = band_owner.shape[0]
    capacity = 3 * band_count // owners
    tx_count = tx_offsets.shape[0]
    bin_count = K1 * K2
    speed_bins = bin_count // SLOTS
    band_width = speed_bins // band_count
    starts = (tx_offsets - speed_bins // 2) % bin_count
    sender = jnp.arange(tx_count, dtype=jnp.int32)[:, None]
    speed = jnp.arange(speed_bins, dtype=jnp.int32)[None, :] - speed_bins // 2
    phase_angle = (sender * speed).astype(jnp.float32) * (-2.0 * math.pi / (tx_count * speed_bins))
    cos_part = jnp.cos(phase_angle)[:, None, None, :]
    sin_part = jnp.sin(phase_angle)[:, None, None, :]
    pieces = lax.all_to_all(samples, "chirp", split_axis=1, concat_axis=3, tiled=True)
    bin_rows = pieces.shape[1]
    item_count = pieces.shape[2]
    spec_re, spec_im = spectrum_of(
        pieces[0].reshape(bin_rows * item_count, bin_count),
        pieces[1].reshape(bin_rows * item_count, bin_count),
        bin_rows * item_count,
    )
    joined = jnp.stack([spec_re, spec_im]).reshape(2, bin_rows, item_count, bin_count)
    double = jnp.concatenate([joined, joined], axis=3)

    def take_band(begin_at):
        return lax.dynamic_slice_in_dim(double, begin_at, speed_bins, 3)

    picked = jax.vmap(take_band)(starts)
    got_re = picked[:, 0].astype(jnp.float32)
    got_im = picked[:, 1].astype(jnp.float32)
    demux_re = got_re * cos_part - got_im * sin_part
    demux_im = got_re * sin_part + got_im * cos_part
    demuxed = jnp.stack([demux_re, demux_im]).astype(jnp.bfloat16)
    demuxed = demuxed.transpose(0, 1, 3, 2, 4)
    rx_local = demuxed.shape[2]
    bin_rows = demuxed.shape[3]
    tile_width = bin_rows * band_width
    tiles = demuxed.reshape(2, tx_count, rx_local, bin_rows, band_count, band_width)
    tiles = tiles.transpose(4, 0, 1, 2, 3, 5).reshape(band_count, 2, tx_count, rx_local, tile_width)
    counter = jnp.arange(band_count, dtype=jnp.int32)
    same_owner = band_owner[:, None] == band_owner[None, :]
    earlier = counter[None, :] < counter[:, None]
    band_rank = jnp.sum((same_owner & earlier).astype(jnp.int32), axis=1)
    weight_re = beam_weights[0]
    weight_im = beam_weights[1]
    slot_ids = band_owner * capacity + band_rank
    choose = (slot_ids[None, :] == jnp.arange(owners * capacity, dtype=jnp.int32)[:, None]).astype(
        jnp.bfloat16
    )
    outgoing = jnp.dot(
        choose, tiles.reshape(band_count, -1), preferred_element_type=jnp.float32
    ).astype(jnp.bfloat16)
    outgoing = outgoing.reshape(owners, capacity, 2, tx_count, rx_local, tile_width)
    slots = lax.all_to_all(outgoing, "rx", split_axis=0, concat_axis=4, tiled=True)[0]
    item_count = slots.shape[0]
    channels = slots.reshape(item_count, 2, slots.shape[2] * slots.shape[3], slots.shape[4])
    mixing = partial(jnp.einsum, preferred_element_type=jnp.float32)
    beam_re = mixing("bc,scm->sbm", weight_re, channels[:, 0]) - mixing(
        "bc,scm->sbm", weight_im, channels[:, 1]
    )
    beam_im = mixing("bc,scm->sbm", weight_re, channels[:, 1]) + mixing(
        "bc,scm->sbm", weight_im, channels[:, 0]
    )
    return jnp.stack([beam_re, beam_im], axis=1).astype(jnp.bfloat16)


LANES = 128
GROUPS = 32


def fourier_of_8(re, im):
    half = math.sqrt(0.5)

    x = list(zip(re, im))
    even = fourier_of_4(x[0], x[2], x[4], x[6])
    odd = fourier_of_4(x[1], x[3], x[5], x[7])
    o1 = ((odd[1][0] + odd[1][1]) * half, (odd[1][1] - odd[1][0]) * half)
    o3 = ((odd[3][1] - odd[3][0]) * half, -(odd[3][0] + odd[3][1]) * half)
    turned = (odd[0], o1, (odd[2][1], -odd[2][0]), o3)
    first = [(e[0] + o[0], e[1] + o[1]) for e, o in zip(even, turned)]
    second = [(e[0] - o[0], e[1] - o[1]) for e, o in zip(even, turned)]
    return first + second


def swap_lanes(tiles):
    tiles = list(tiles)
    lane = lax.broadcasted_iota(jnp.int32, tiles[0].shape, 1)
    width = LANES // 2
    step = len(tiles) // 2
    while step:
        keep = lane // width % 2 == 0
        for i in range(len(tiles)):
            if i // step % 2 == 0:
                a, b = tiles[i], tiles[i + step]
                tiles[i] = jnp.where(keep, a, pltpu.roll(b, width, 1))
                tiles[i + step] = jnp.where(keep, pltpu.roll(a, LANES - width, 1), b)
        width //= 2
        step //= 2
    return tiles


def fourier_of_4(a, b, c, d):
    s0, s1 = (a[0] + c[0], a[1] + c[1]), (a[0] - c[0], a[1] - c[1])
    s2, s3 = (b[0] + d[0], b[1] + d[1]), (b[0] - d[0], b[1] - d[1])
    return (
        (s0[0] + s2[0], s0[1] + s2[1]),
        (s1[0] + s3[1], s1[1] - s3[0]),
        (s0[0] - s2[0], s0[1] - s2[1]),
        (s1[0] - s3[1], s1[1] + s3[0]),
    )


def beams_kernel(owners, sources, skip, near, far, first, samples_ref, *refs):
    pieces = refs[: sources - 1]
    table_hbm, weight_hbm = refs[sources - 1 : sources + 1]
    outs = refs[sources + 1 : sources + 1 + owners]
    x, table, weight, part, mixed, spread, packed, staged, x_sem, in_sem, out_sem = refs[
        sources + 1 + owners :
    ]
    chunk_bins, rows = x.shape[2], x.shape[3]
    folds = x.shape[4] // LANES
    tx2 = spread.shape[0]
    halves = rows // 16

    own = samples_ref.at[:, pl.ds(first[0], chunk_bins)]
    here = first[1]
    loads = [pltpu.make_async_copy(own, x.at[here], x_sem.at[0])]
    for c in range(1, sources):
        piece = pieces[c - 1].at[:, pl.ds(skip, chunk_bins)]
        loads.append(pltpu.make_async_copy(piece, x.at[here ^ c], x_sem.at[c]))
    load_table = pltpu.make_async_copy(table_hbm, table, in_sem.at[0])
    load_weight = pltpu.make_async_copy(weight_hbm, weight, in_sem.at[1])
    for load in loads:
        load.start()
    load_table.start()
    load_weight.start()
    for load in loads:
        load.wait()

    def transform(step, carry):
        q = step // halves
        r0 = pl.multiple_of((step % halves) * 16, 16)
        for fold in range(folds):
            span = slice(fold * LANES, (fold + 1) * LANES)
            re = [x[c, 0, q, pl.ds(r0, 16), span].astype(jnp.float32) for c in range(sources)]
            im = [x[c, 1, q, pl.ds(r0, 16), span].astype(jnp.float32) for c in range(sources)]
            for k, (a, b) in enumerate(fourier_of_8(re, im)):
                if fold * k:
                    angle = -2.0 * math.pi * fold * k / GROUPS
                    c, s = math.cos(angle), math.sin(angle)
                    a, b = a * c - b * s, a * s + b * c
                part[fold, k, 0] = a
                part[fold, k, 1] = b
        base = pl.multiple_of(q * rows + r0, 16)
        for k in range(sources):
            quarter = fourier_of_4(*((part[f, k, 0], part[f, k, 1]) for f in range(folds)))
            for f, (a, b) in enumerate(quarter):
                mixed[k + sources * f, pl.ds(base, 16), :LANES] = a.astype(jnp.bfloat16)
                mixed[k + sources * f, pl.ds(base, 16), LANES:] = b.astype(jnp.bfloat16)
        return carry

    lax.fori_loop(0, chunk_bins * halves, transform, 0)
    load_table.wait()

    def demultiplex(group, carry):
        got = lax.dot_general(
            table[group], mixed[group], (((1,), (1,)), ((), ())),
            preferred_element_type=jnp.float32,
        )
        for t in range(tx2):
            spread[t, pl.ds(group, 8, stride=GROUPS), :] = got[8 * t : 8 * t + 8]
        return carry

    lax.fori_loop(0, GROUPS, demultiplex, 0, unroll=16)

    def regroup(band, carry):
        at = pl.multiple_of(band * 16, 16)
        for t in range(tx2 // 4):
            tiles = swap_lanes([spread[4 * t + i, pl.ds(at, 16), :] for i in range(4)])
            for q in range(chunk_bins):
                to = pl.multiple_of((band * chunk_bins + q) * 16, 16)
                packed[pl.ds(to, 16), t * LANES : (t + 1) * LANES] = tiles[q].astype(jnp.bfloat16)
        return carry

    lax.fori_loop(0, 16, regroup, 0, unroll=2)
    load_weight.wait()

    def send(band):
        for k in range(owners):
            @pl.when(near[band] == k)
            def _():
                pltpu.make_async_copy(
                    staged.at[band], outs[k].at[far[band]], out_sem.at[band]
                ).start()

    parts = LANES // 16 // chunk_bins
    height = 512 // parts
    for block in range(chunk_bins):
        beams = lax.dot_general(
            weight[...], packed[256 * block : 256 * block + 256], (((1,), (1,)), ((), ())),
            preferred_element_type=jnp.float32,
        )
        for pair in range(2):
            lanes = slice(pair * LANES, (pair + 1) * LANES)
            tiles = swap_lanes(
                [beams[height * p : height * p + height, lanes] for p in range(parts)]
            )
            for side in range(parts):
                band = (2 * block + pair) * parts + side
                staged[band] = tiles[side].astype(jnp.bfloat16)
                send(band)
    for band in range(16):
        pltpu.make_async_copy(staged.at[band], outs[0].at[0], out_sem.at[band]).wait()


def beams_of(
    near, far, first, samples, pieces, skip, count, table, weights, owners, capacity
):
    sources = len(pieces) + 1
    piece = (2, count) + pieces[0].shape[2:]
    share = (512 * 16 * piece[1] // LANES, LANES)
    tx2 = table.shape[1] // 8
    smem = pl.BlockSpec(memory_space=pltpu.SMEM)
    hbm = pl.BlockSpec(memory_space=pl.ANY)
    return pl.pallas_call(
        partial(beams_kernel, owners, sources, skip),
        out_shape=[jax.ShapeDtypeStruct((capacity, *share), jnp.bfloat16)] * owners,
        in_specs=[smem] * 3 + [hbm] * (sources + 2),
        out_specs=[hbm] * owners,
        scratch_shapes=[
            pltpu.VMEM((sources,) + piece, jnp.bfloat16),
            pltpu.VMEM(table.shape, jnp.bfloat16),
            pltpu.VMEM(weights.shape, jnp.bfloat16),
            pltpu.VMEM((4, 8, 2, 16, LANES), jnp.float32),
            pltpu.VMEM((GROUPS, LANES, 2 * LANES), jnp.bfloat16),
            pltpu.VMEM((tx2, 256, LANES), jnp.float32),
            pltpu.VMEM((256 * piece[1], tx2 // 4 * LANES), jnp.bfloat16),
            pltpu.VMEM((16, *share), jnp.bfloat16),
            pltpu.SemaphoreType.DMA((sources,)),
            pltpu.SemaphoreType.DMA((2,)),
            pltpu.SemaphoreType.DMA((16,)),
        ],
        compiler_params=pltpu.CompilerParams(vmem_limit_bytes=40 << 20),
        name="beams",
    )(near, far, first, samples, *pieces, table, weights)


STORE_SLOTS = 6
ORDER = (1, 2, 3, 6, 7, 4, 5)
EXCHANGED = ((0, 6), (8, 4), (12, 4), (6, 2))
COMPUTED = ((0, 0, 4), (0, 4, 2), (1, 0, 4), (2, 0, 4), (3, 0, 2))
TILES = ((0, 1, 4), (2, 3))


def store_kernel(owners, taken, mine, me, *refs):
    chunks = (len(refs) - 2) // (owners + 1)
    sources, out_ref = refs[: chunks * owners], refs[chunks * owners]
    held, sem = refs[-1 - chunks : -1], refs[-1]
    lane = lax.broadcasted_iota(jnp.int32, (128, LANES), 1)

    @pl.when(pl.program_id(0) == 0)
    def _():
        loads = []
        for c in range(chunks):
            for k in range(owners):
                source = sources[c * owners + k]
                count = source.shape[0]
                to = held[c].at[pl.ds((me[0] ^ k) * count, count)]
                loads.append(pltpu.make_async_copy(source, to, sem.at[c * owners + k]))
        for load in loads:
            load.start()
        for load in loads:
            load.wait()

    for s in range(STORE_SLOTS):
        slot = pl.program_id(0) * STORE_SLOTS + s
        used = slot < taken[0]
        tiles = [ref[mine[slot]].astype(jnp.float32) for ref in held]
        for quarter in range(4):
            tile, start = None, 0
            for total in tiles:
                per_part = total.shape[0] // 128
                part, inner = quarter // per_part, quarter % per_part
                width = 32 * per_part
                piece = total[128 * inner : 128 * inner + 128]
                shift = (start - part * width) % LANES
                piece = pltpu.roll(piece, shift, 1) if shift else piece
                tile = piece if tile is None else jnp.where(lane < start, tile, piece)
                start += width
            tile = jnp.where(used, tile, 0.0).astype(jnp.bfloat16)
            out_ref[s, 0, 64 * quarter : 64 * quarter + 64, :] = tile[:64]
            out_ref[s, 1, 64 * quarter : 64 * quarter + 64, :] = tile[64:]


def store_tile(taken, mine, me, chunks, so_far, tile, capacity):
    owners = len(chunks[0])
    args = [share for chunk in chunks for share in chunk]
    count = len(args)
    hbm = pl.BlockSpec(memory_space=pl.ANY)
    aliases = {}
    if so_far is not None:
        args.append(so_far)
        aliases = {3 + count: 0}

    def body(taken, mine, me, *refs):
        store_kernel(owners, taken, mine, me, *refs[:count], *refs[len(args) :])

    return pl.pallas_call(
        body,
        out_shape=jax.ShapeDtypeStruct((capacity, 2, 256, 2 * LANES), jnp.bfloat16),
        grid_spec=pltpu.PrefetchScalarGridSpec(
            num_scalar_prefetch=3,
            grid=(capacity // STORE_SLOTS,),
            in_specs=[hbm] * len(args),
            out_specs=pl.BlockSpec((STORE_SLOTS, 2, 256, LANES), lambda s, *_: (s, 0, 0, tile)),
            scratch_shapes=[
                pltpu.VMEM((owners * chunk[0].shape[0],) + chunk[0].shape[1:], jnp.bfloat16)
                for chunk in chunks
            ]
            + [pltpu.SemaphoreType.DMA((count,))],
        ),
        input_output_aliases=aliases,
        name="store",
    )(taken, mine, me, *args)


def tuned(samples, tx_offsets, band_owner, beam_weights):
    owners = lax.axis_size("rx")
    spans = lax.axis_size("chirp")
    me = lax.axis_index("rx")
    bands = band_owner.shape[0]
    tx_count = tx_offsets.shape[0]
    capacity = 3 * bands // owners
    rows = samples.shape[2]
    bins = samples.shape[1] // spans

    counter = jnp.arange(bands, dtype=jnp.int32)
    same_owner = band_owner[:, None] == band_owner[None, :]
    earlier = counter[None, :] < counter[:, None]
    band_rank = jnp.sum((same_owner & earlier).astype(jnp.int32), axis=1)
    summed = bands // owners
    near = counter // summed ^ me
    far = counter % summed
    is_mine = band_owner == me
    taken = jnp.sum(is_mine.astype(jnp.int32)).reshape(1)
    slot = jnp.arange(capacity, dtype=jnp.int32)[:, None]
    mine = jnp.sum(jnp.where((band_rank == slot) & is_mine, counter, 0), axis=1).astype(jnp.int32)

    here = lax.axis_index("chirp")
    two_pi = 2.0 * math.pi
    group = jnp.arange(GROUPS, dtype=jnp.int32)
    high = jnp.arange(8, dtype=jnp.int32)
    lane = jnp.arange(LANES, dtype=jnp.int32)
    sender = jnp.arange(tx_count, dtype=jnp.int32)
    start = tx_offsets[:, None] + 32 * high[None, :] + 4096 - 128
    a1 = (start[:, :, None] * lane % 4096).astype(jnp.float32) * (-two_pi / 4096)
    a2 = (group[:, None] * lane[None, :]).astype(jnp.float32) * (-two_pi / 4096)
    speed = 32 * high[None, :] + group[:, None] - 128
    a3 = (sender[None, :, None] * speed[:, None, :]).astype(jnp.float32) * (
        -two_pi / (tx_count * 256)
    )
    c1, s1 = lax.optimization_barrier((jnp.cos(a1), jnp.sin(a1)))
    c2, s2 = lax.optimization_barrier((jnp.cos(a2) / 64, jnp.sin(a2) / 64))
    c3, s3 = lax.optimization_barrier((jnp.cos(a3), jnp.sin(a3)))
    c2, s2 = c2[:, None, None, :], s2[:, None, None, :]
    c3, s3 = c3[..., None], s3[..., None]
    c12, s12 = c1 * c2 - s1 * s2, c1 * s2 + s1 * c2
    turn_re = (c12 * c3 - s12 * s3).reshape(GROUPS, tx_count * 8, LANES)
    turn_im = (c12 * s3 + s12 * c3).reshape(GROUPS, tx_count * 8, LANES)
    table = jnp.concatenate(
        [
            jnp.concatenate([turn_re, -turn_im], axis=2),
            jnp.concatenate([turn_im, turn_re], axis=2),
        ],
        axis=1,
    ).astype(jnp.bfloat16)

    local = lax.dynamic_slice_in_dim(
        beam_weights.reshape(2, 4, 64, tx_count, owners * rows), me * rows, rows, 4
    )
    local = local.reshape(2, 4, 64, tx_count * rows)
    weights = jnp.stack(
        [
            jnp.concatenate([local[0], -local[1]], axis=2),
            jnp.concatenate([local[1], local[0]], axis=2),
        ],
        axis=1,
    ).reshape(512, 2 * tx_count * rows)

    crossings = [[(i, i ^ k) for i in range(spans)] for k in range(spans)]
    swaps = [[(i, i ^ k) for i in range(owners)] for k in range(owners)]
    blocks = [
        [
            lax.dynamic_slice_in_dim(samples, (here ^ k) * bins + offset, count, 1)
            for k in range(1, spans)
        ]
        for offset, count in EXCHANGED
    ]
    arrived = []
    for parts in blocks:
        got = {}
        for k in ORDER:
            got[k] = lax.ppermute(parts[k - 1], "chirp", crossings[k])
        arrived.append([got[k] for k in range(1, spans)])

    shares = []
    for which, skip, count in COMPUTED:
        at = jnp.stack([here * bins + EXCHANGED[which][0] + skip, here]).astype(jnp.int32)
        shares.append(
            beams_of(
                near, far, at, samples, arrived[which], skip, count, table, weights, owners, summed,
            )
        )

    def to_others(blocks):
        got = {}
        for k in reversed(range(1, owners)):
            got[k] = lax.ppermute(blocks[k], "rx", swaps[k])
        return [blocks[0]] + [got[k] for k in range(1, owners)]

    groups = []
    for share in shares:
        parts = [part.astype(jnp.float32) for part in to_others(share)]
        total = sum(parts[1:], parts[0]).astype(jnp.bfloat16)
        groups.append(to_others([total] * owners))
    store = None
    for tile in sorted(range(len(TILES)), reverse=True):
        chunks = [groups[i] for i in TILES[tile]]
        store = store_tile(taken, mine, me.reshape(1), chunks, store, tile, capacity)
    return store


def shards(samples, tx_offsets, band_owner, beam_weights):
    fits = (
        lax.axis_size("rx") == 4
        and lax.axis_size("chirp") == 8
        and samples.shape == (2, 128, 32, 512)
        and beam_weights.shape == (2, 256, 1536)
    )
    if fits:
        return tuned(samples, tx_offsets, band_owner, beam_weights)
    return general(samples, tx_offsets, band_owner, beam_weights)


def solution(mesh):
    placed = (P(None, None, "rx", "chirp"), P(), P(), P())
    step = jax.shard_map(
        shards, mesh=mesh, in_specs=placed, out_specs=P("rx", None, None, "chirp"), check_vma=False
    )
    if dict(mesh.shape) != {"rx": 4, "chirp": 8}:
        return step
    return step
```
